32 devices in a mesh: dp: 4 (over y, x), fsdp: 8 (over z, core).
Axes of the slice: x: 2, y: 2, z: 4, core: 2. Of those that a mesh axis runs over, the one named last changes fastest.
Arguments:
- tokens: float32 [32768, 4096], P(('dp', 'fsdp')), may hold values from -6 to 6
- curvature: float32 [32768, 512], P(('dp', 'fsdp')), may hold values from 0.05 to 1
- values: float32 [4096, 512], P('fsdp'), may hold values from -6 to 6
- input_basis: float32 [4096, 4096], P(None, ('dp', 'fsdp')), may hold values from -1 to 1, as said below
- output_basis: float32 [512, 512], replicated, may hold values from -1 to 1, as said below
- eigenvalues: float32 [4096, 512], P(('dp', 'fsdp')), may hold values from 0.3 to 3
Outputs:
- stepped: float32 [4096, 512], P('fsdp')
The draws below stay inside these ranges and needn't reach their ends.
Inputs may be any that keep to these rules, and one draw needn't show every extreme that they name: `input_basis`: an orthogonal 4096 x 4096 matrix. `output_basis`: an orthogonal 512 x 512 matrix.
All inputs are finite; a program needn't handle non-finite values.
Results may differ from the reference program's by a relative error of at most 0.000071.
Values sent between devices are 32-bit elements; how exact they have to be, the bound alone decides.
No kernel may reach another device: no remote copies, remote signals or barrier semaphores. Data moves between devices by JAX's collectives and lax.ppermute only.
A program may use at most 128 MiB of HBM per device.

```python
import math
import jax
import jax.numpy as jnp
from jax import lax

D = 4096
KV = 512
TOKENS = 32768


def draw_input_basis(key, part):
    matrix = jax.random.normal(jax.random.fold_in(key, 11), (D, D), jnp.float32)
    orthogonal, upper = jnp.linalg.qr(matrix)
    return orthogonal


def draw_output_basis(key, part):
    matrix = jax.random.normal(jax.random.fold_in(key, 23), (KV, KV), jnp.float32)
    orthogonal, upper = jnp.linalg.qr(matrix)
    return orthogonal


def levels(own_key, dims, split, least, top_value):
    factor_of = 1.0
    for position, shards_of in split:
        heights = jax.random.uniform(jax.random.fold_in(jax.random.fold_in(own_key, 6), position), (shards_of,), jnp.float32, least / len(split), top_value / len(split))
        factor_of = factor_of * jnp.repeat(jnp.exp(heights), dims[position] // shards_of).reshape((-1,) + (1,) * (len(dims) - 1 - position))
    return factor_of


def centred(own_key, dims, spread, bound, cuts=(), dtype=jnp.bfloat16):
    values = spread * jax.random.normal(own_key, dims, jnp.float32)
    if cuts:
        values = values * levels(own_key, dims, cuts, -0.22, 0.18)
    return jnp.clip(values, -bound, bound).astype(dtype)


def setup_inputs(seed: int = 0) -> dict:
    seeds = jax.random.split(jax.random.key(seed), 7)
    return {
        "tokens": centred(seeds[0], (TOKENS, D), 1.0, 6.0, ((0, 32),), jnp.float32),
        "curvature": jnp.clip(jnp.exp(math.log(1.0) - 2.9957323 * jax.random.uniform(seeds[1], (TOKENS, KV), jnp.float32) ** levels(seeds[1], (TOKENS, KV), ((0, 32),), -0.2, 0.2)), 0.05, 1.0),
        "values": centred(seeds[2], (D, KV), 1.0, 6.0, ((0, 8),), jnp.float32),
        "input_basis": draw_input_basis(jax.random.fold_in(seeds[6], 71), 0),
        "output_basis": draw_output_basis(jax.random.fold_in(seeds[6], 71), 0),
        "eigenvalues": jnp.clip(jnp.exp(math.log(3.0) - 2.3025851 * jax.random.uniform(seeds[5], (D, KV), jnp.float32) ** levels(seeds[5], (D, KV), ((0, 32),), -0.2, 0.2)), 0.3, 3.0),
    }


def reference(tokens, curvature, values, input_basis, output_basis, eigenvalues):
    highest = lax.Precision.HIGHEST
    projected = jnp.dot(tokens.astype(jnp.float32), values.astype(jnp.float32), precision=highest, preferred_element_type=jnp.float32)
    weighted = curvature * projected
    moment = jnp.dot(tokens.T.astype(jnp.float32), weighted.astype(jnp.float32), precision=highest, preferred_element_type=jnp.float32) / TOKENS
    rotated = jnp.dot(jnp.dot(input_basis.T.astype(jnp.float32), moment.astype(jnp.float32), precision=highest, preferred_element_type=jnp.float32).astype(jnp.float32), output_basis.astype(jnp.float32), precision=highest, preferred_element_type=jnp.float32)
    scaled = rotated / eigenvalues
    update = jnp.dot(jnp.dot(input_basis.astype(jnp.float32), scaled.astype(jnp.float32), precision=highest, preferred_element_type=jnp.float32).astype(jnp.float32), output_basis.T.astype(jnp.float32), precision=highest, preferred_element_type=jnp.float32)
    return values - update
```

```python
import functools

import jax
import jax.numpy as jnp
from jax import lax
from jax.experimental import pallas as pl
from jax.experimental.pallas import tpu as pltpu
from jax.sharding import PartitionSpec as P


VMEM_LIMIT = 40 * 1024 * 1024
F32 = jnp.float32
BF16 = jnp.bfloat16


def split(x):
    high = x.astype(BF16)
    return high, (x - high.astype(F32)).astype(BF16)


def dot3(a, b, dims):
    contract = (dims, ((), ()))
    dot = functools.partial(lax.dot_general, dimension_numbers=contract, preferred_element_type=F32)
    return dot(a[0], b[0]) + (dot(a[0], b[1]) + dot(a[1], b[0]))


NN = ((1,), (0,))
TN = ((0,), (0,))
NT = ((1,), (1,))


def cost(flops, bytes_accessed):
    return pl.CostEstimate(flops=flops, bytes_accessed=bytes_accessed, transcendentals=0)


def params():
    return pltpu.CompilerParams(vmem_limit_bytes=VMEM_LIMIT)


def whole(shape):
    return pl.BlockSpec(shape, lambda *_: (0,) * len(shape))


def project(tokens, pieces, index, accumulator, finish, rows=256):
    count = len(pieces[0])
    piece_rows, outputs = pieces[0][0].shape
    half = count * piece_rows
    depth = 2 * half
    local = tokens.shape[0]
    with_acc = accumulator is not None

    def body(s, t_ref, *refs):
        refs = list(refs)
        own, other = refs[:count], refs[count : 2 * count]
        refs = refs[2 * count :]
        acc_ref = refs.pop(0) if with_acc else None
        curvature_ref = refs.pop(0) if finish is not None else None
        high_ref, low_ref = refs[-2:]
        outs = refs[:-2]

        @pl.when(pl.program_id(0) == 0)
        def _():
            for core, group in ((s[1], own), (1 - s[1], other)):
                for k, ref in enumerate(group):
                    at = pl.ds(pl.multiple_of(core * half + s[2 + k] * piece_rows, piece_rows), piece_rows)
                    high_ref[at, :], low_ref[at, :] = split(ref[...])

        total = dot3(split(t_ref[...]), (high_ref[...], low_ref[...]), NN)
        if with_acc:
            total = total + acc_ref[...]
        if finish is None:
            outs[0][...] = total
        else:
            outs[0][...], outs[1][...] = split(total * curvature_ref[...] * finish[1])

    tile = pl.BlockSpec((rows, outputs), lambda i, s: (i, 0))
    flat = list(pieces[0]) + list(pieces[1])
    specs = [pl.BlockSpec((rows, depth), lambda i, s: (i, s[0]))]
    specs += [whole((piece_rows, outputs))] * len(flat)
    operands = [tokens] + flat
    aliases = {}
    if with_acc:
        specs.append(tile)
        operands.append(accumulator)
        if finish is None:
            aliases = {len(operands): 0}
    if finish is not None:
        specs.append(tile)
        operands.append(finish[0])
    dtypes = (F32,) if finish is None else (BF16, BF16)
    return pl.pallas_call(
        body,
        grid_spec=pltpu.PrefetchScalarGridSpec(
            num_scalar_prefetch=1,
            grid=(local // rows,),
            in_specs=specs,
            out_specs=[tile] * len(dtypes),
            scratch_shapes=[pltpu.VMEM((depth, outputs), BF16)] * 2,
        ),
        out_shape=[jax.ShapeDtypeStruct((local, outputs), dtype) for dtype in dtypes],
        input_output_aliases=aliases,
        compiler_params=params(),
        cost_estimate=cost(6 * local * depth * outputs, 4 * local * (depth + 2 * outputs)),
        name="project",
    )(index, *operands)


def moment_block(tokens, weighted, index, width, extra, pieces):
    local = tokens.shape[0]
    outputs = weighted[0].shape[1]
    steps = 2 if width % 256 == 0 else 1
    part = width // steps
    piece_rows = width // pieces

    def body(s, t_ref, high_ref, low_ref, *refs):
        refs = list(refs)
        extra_ref = refs.pop(0) if extra is not None else None
        total_ref = refs.pop() if pieces > 1 else refs[0]
        step = pl.program_id(0)
        at = pl.ds(pl.multiple_of(step * part, part), part)
        value = dot3(split(t_ref[...]), (high_ref[...], low_ref[...]), TN)
        if extra is not None:
            value = value + extra_ref[at, :]
        total_ref[at, :] = value
        if pieces > 1:

            @pl.when(step == steps - 1)
            def _():
                for k, ref in enumerate(refs):
                    ref[...] = total_ref[pl.ds(pl.multiple_of(s[1 + k] * piece_rows, piece_rows), piece_rows), :]

    specs = [
        pl.BlockSpec((local, part), lambda i, s: (0, s[0] * steps + i)),
        whole((local, outputs)),
        whole((local, outputs)),
    ]
    operands = [tokens, *weighted]
    if extra is not None:
        specs.append(whole((width, outputs)))
        operands.append(extra)
    return pl.pallas_call(
        body,
        grid_spec=pltpu.PrefetchScalarGridSpec(
            num_scalar_prefetch=1,
            grid=(steps,),
            in_specs=specs,
            out_specs=[whole((piece_rows, outputs))] * pieces,
            scratch_shapes=[pltpu.VMEM((width, outputs), F32)] if pieces > 1 else [],
        ),
        out_shape=[jax.ShapeDtypeStruct((piece_rows, outputs), F32)] * pieces,
        compiler_params=params(),
        cost_estimate=cost(6 * local * width * outputs, 4 * local * (width + outputs)),
        name="moment",
    )(index, *operands)


def rotate_left(bases, moments, index, extras):
    count = len(bases)
    depth, width = bases[0].shape
    piece_rows, outputs = moments[0].shape

    def body(s, *refs):
        basis_refs, refs = refs[:count], refs[count:]
        moment_refs, refs = refs[: len(moments)], refs[len(moments) :]
        extra_ref = refs[0] if extras is not None else None
        high_ref, low_ref = refs[-2:]
        outs = refs[1:-2] if extras is not None else refs[:-2]
        for k, ref in enumerate(moment_refs):
            at = pl.ds(pl.multiple_of(s[k] * piece_rows, piece_rows), piece_rows)
            high_ref[at, :], low_ref[at, :] = split(ref[...])
        moment = high_ref[...], low_ref[...]
        for k, ref in enumerate(basis_refs):
            value = dot3(split(ref[...]), moment, TN)
            if extras is None:
                outs[0][k] = value
            else:
                outs[k][...] = value + extra_ref[k]

    specs = [whole((depth, width))] * count + [whole((piece_rows, outputs))] * len(moments)
    operands = list(bases) + list(moments)
    if extras is None:
        shapes = [(count, width, outputs)]
    else:
        specs.append(whole((count, width, outputs)))
        operands.append(extras)
        shapes = [(width, outputs)] * count
    return pl.pallas_call(
        body,
        grid_spec=pltpu.PrefetchScalarGridSpec(
            num_scalar_prefetch=1,
            grid=(1,),
            in_specs=specs,
            out_specs=[whole(shape) for shape in shapes],
            scratch_shapes=[pltpu.VMEM((depth, outputs), BF16)] * 2,
        ),
        out_shape=[jax.ShapeDtypeStruct(shape, F32) for shape in shapes],
        compiler_params=params(),
        cost_estimate=cost(6 * depth * width * count * outputs, 8 * depth * (count * width + outputs)),
        name="rotate_left",
    )(index, *operands)


def scale(parts, output_basis, eigenvalues):
    def body(*refs):
        part_refs = refs[: len(parts)]
        basis_ref, eigen_ref, out_ref = refs[len(parts) :]
        left = part_refs[0][...]
        for ref in part_refs[1:]:
            left = left + ref[...]
        basis = split(basis_ref[...])
        scaled = dot3(split(left), basis, NN) / eigen_ref[...]
        out_ref[...] = dot3(split(scaled), basis, NT)

    return pl.pallas_call(
        body,
        out_shape=jax.ShapeDtypeStruct(eigenvalues.shape, F32),
        compiler_params=params(),
        cost_estimate=cost(12 * eigenvalues.size * output_basis.shape[0], 4 * output_basis.size),
        name="scale",
    )(*parts, output_basis, eigenvalues)


def rotate_back(bases, mapped, index, pieces):
    count = len(bases)
    depth, width = bases[0].shape
    outputs = mapped[0].shape[1]
    piece_rows = depth // pieces

    def body(s, *refs):
        basis_refs, mapped_refs = refs[:count], refs[count : 2 * count]
        outs, total_ref = refs[2 * count : -1], refs[-1]
        total = None
        for basis_ref, mapped_ref in zip(basis_refs, mapped_refs):
            value = dot3(split(basis_ref[...]), split(mapped_ref[...]), NN)
            total = value if total is None else total + value
        total_ref[...] = total
        for k, ref in enumerate(outs):
            ref[...] = total_ref[pl.ds(pl.multiple_of(s[k] * piece_rows, piece_rows), piece_rows), :]

    return pl.pallas_call(
        body,
        grid_spec=pltpu.PrefetchScalarGridSpec(
            num_scalar_prefetch=1,
            grid=(1,),
            in_specs=[whole((depth, width))] * count + [whole((width, outputs))] * count,
            out_specs=[whole((piece_rows, outputs))] * pieces,
            scratch_shapes=[pltpu.VMEM((depth, outputs), F32)],
        ),
        out_shape=[jax.ShapeDtypeStruct((piece_rows, outputs), F32)] * pieces,
        compiler_params=params(),
        cost_estimate=cost(6 * depth * width * count * outputs, 8 * depth * (count * width + outputs)),
        name="rotate_back",
    )(index, *bases, *mapped)


def assemble(parts, index):
    piece_rows, outputs = parts[0].shape

    def body(s, *refs):
        for k, ref in enumerate(refs[:-1]):
            refs[-1][pl.ds(pl.multiple_of(s[k] * piece_rows, piece_rows), piece_rows), :] = ref[...]

    shape = (piece_rows * len(parts), outputs)
    return pl.pallas_call(
        body,
        grid_spec=pltpu.PrefetchScalarGridSpec(
            num_scalar_prefetch=1,
            grid=(1,),
            in_specs=[whole((piece_rows, outputs))] * len(parts),
            out_specs=whole(shape),
        ),
        out_shape=jax.ShapeDtypeStruct(shape, F32),
        compiler_params=params(),
        cost_estimate=cost(0, 8 * piece_rows * len(parts) * outputs),
        name="assemble",
    )(index, *parts)


def add(parts):
    total = parts[0]
    for part in parts[1:]:
        total = total + part
    return total


def body(tokens, curvature, values, input_basis, output_basis, eigenvalues):
    groups, members = lax.axis_size("dp"), lax.axis_size("fsdp")
    chips = members // 2
    d, f = lax.axis_index("dp").astype(jnp.int32), lax.axis_index("fsdp").astype(jnp.int32)
    z, c = f // 2, f % 2
    rows = values.shape[0]
    piece = rows // groups
    inverse_total = 1.0 / (tokens.shape[0] * groups * members)

    def over_dp(x, k):
        return lax.ppermute(x, "dp", [(a, a ^ k) for a in range(groups)])

    def over_fsdp(x, j):
        return lax.ppermute(x, "fsdp", [(a, a ^ j) for a in range(members)])

    places = [d ^ k for k in range(groups)]
    place_index = jnp.stack(places)

    def after(x, anchor):
        return lax.optimization_barrier((x, anchor))[0]

    quarter = lax.dynamic_slice_in_dim(values, d * piece, piece, 0)
    columns = [over_fsdp(quarter, 2 * j) for j in range(1, chips)]
    own = [[values]] + [[x] + [over_dp(x, k) for k in range(1, groups)] for x in columns]
    other = [[over_fsdp(x, 1) for x in group] for group in own]
    accumulator = None
    for j in range(chips):
        places_of = [jnp.int32(0)] if j == 0 else places
        index = jnp.stack([z ^ j, c] + places_of)
        finish = (curvature, inverse_total) if j == chips - 1 else None
        result = project(tokens, (own[j], other[j]), index, accumulator, finish)
        accumulator = result[0]
    weighted = result

    basis_source = after(input_basis, columns[0])
    bases = []
    for j in range(members):
        block = lax.dynamic_slice_in_dim(basis_source, (f ^ j) * rows, rows, 0)
        bases.append(block if j == 0 else over_fsdp(block, j))

    order = list(range(chips - 1, -1, -1))
    crossing = {}

    def cross(j):
        index = jnp.stack([f ^ (2 * j + 1)])
        crossing[j] = over_fsdp(moment_block(tokens, weighted, index, rows, None, 1)[0], 1)

    cross(order[0])
    sums = []
    for at, j in enumerate(order):
        if at + 1 < chips:
            cross(order[at + 1])
        index = jnp.stack([f ^ (2 * j)] + places)
        parts = moment_block(tokens, weighted, index, rows, crossing[j], groups)
        received = [parts[0]] + [over_dp(parts[k], k) for k in range(1, groups)]
        if j:
            sums.append(over_fsdp(add(received), 2 * j))
        else:
            sums += received
    moment = add(sums)

    moments = [moment] + [over_dp(moment, k) for k in range(1, groups)]
    crossed = over_fsdp(rotate_left(bases[1::2], moments, place_index, None)[0], 1)
    lefts = rotate_left(bases[0::2], moments, place_index, crossed)
    lefts = [lefts[0]] + [over_fsdp(lefts[j], 2 * j) for j in range(1, chips)]
    mapped = scale(lefts, output_basis, eigenvalues)
    evens = [mapped] + [over_fsdp(mapped, 2 * j) for j in range(1, chips)]
    odds = [over_fsdp(x, 1) for x in evens]
    updates = rotate_back(bases, [x for pair in zip(evens, odds) for x in pair], place_index, groups)
    update = add([updates[0]] + [over_dp(updates[k], k) for k in range(1, groups)])
    stepped = quarter - update
    return assemble([stepped] + [over_dp(stepped, k) for k in range(1, groups)], place_index)


def solution(mesh):
    placed = (
        P(("dp", "fsdp"), None),
        P(("dp", "fsdp"), None),
        P("fsdp", None),
        P(None, ("dp", "fsdp")),
        P(),
        P(("dp", "fsdp"), None),
    )
    return jax.shard_map(
        body, mesh=mesh, in_specs=placed, out_specs=P("fsdp", None), check_vma=False
    )
```
